256 devices in a mesh: samp: 16 (over y_hi, x, core), head: 16 (over y_lo, z).
Axes of the slice: x: 4, y: 4 (y_hi: 2, y_lo: 2; y = y_hi * 2 + y_lo), z: 8, core: 2. Of those that a mesh axis runs over, the one named last changes fastest.
Arguments:
- input_tokens: bfloat16 [32, 512, 768], P('samp'), may hold values from -6 to 6
- output_cotangent: bfloat16 [32, 512, 768], P('samp'), may hold values from -15 to 15
- query_weight: bfloat16 [768, 768], P(None, 'head'), may hold values from -0.21875 to 0.21875
- key_weight: bfloat16 [768, 768], P(None, 'head'), may hold values from -0.21875 to 0.21875
- value_weight: bfloat16 [768, 768], P(None, 'head'), may hold values from -0.21875 to 0.21875
- output_weight: bfloat16 [768, 768], P('head'), may hold values from -0.21875 to 0.21875
- pair_bias: bfloat16 [16, 512, 512], P('head'), may hold values from -6 to 240
- valid_len: int32 [1], replicated, may hold values from 256 to 512
- pair_in: bfloat16 [512, 512, 128], P('head', 'samp'), may hold values from -6 to 6
- w_bias: bfloat16 [128, 16], replicated, may hold values from -6 to 6
- t_gate: bfloat16 [2, 128, 256], replicated, may hold values from -0.5 to 0.5
- t_up: bfloat16 [2, 128, 256], replicated, may hold values from -0.5 to 0.5
- t_down: bfloat16 [2, 256, 128], replicated, may hold values from -0.375 to 0.375
Outputs:
- d_tokens: bfloat16 [32, 512, 768], P('samp', None, 'head')
- d_pair: bfloat16 [512, 512, 128], P('head', 'samp')
- d_trans_gate: float32 [2, 128, 256], replicated
- d_trans_up: float32 [2, 128, 256], replicated
- d_trans_down: float32 [2, 256, 128], replicated
The draws below stay inside these ranges and needn't reach their ends.
All inputs are finite; a program needn't handle non-finite values.
Results may differ from the reference program's by a relative error of at most 0.02.
Values may be sent and summed in bfloat16 or wider, within the bound.
No kernel may reach another device: no remote copies, remote signals or barrier semaphores. Data moves between devices by JAX's collectives and lax.ppermute only.
A program may use at most 64 MiB of HBM per device.

```python
import math
import jax
import jax.numpy as jnp
from jax import lax

D = 768
HEADS = 16
HD = 48
CZ = 128
FF = 256
LAYERS = 2
TOKENS = 512
SAMP_DEV = 2
SAMPLES = 32
N_HEAD = 16


def draw_pair_bias(key, part):
    key_base = jax.random.fold_in(jax.random.fold_in(key, 7), 0)
    full_shape = (HEADS, TOKENS, TOKENS)
    bias_field = jnp.clip(jax.random.normal(key_base, full_shape, jnp.float32), -6.0, 6.0)
    return bias_field.astype(jnp.bfloat16)


def level_of(key, shape, shards, least, high):
    gain = 1.0
    for dim, blocks in shards:
        heights = jax.random.uniform(jax.random.fold_in(jax.random.fold_in(key, 6), dim), (blocks,), jnp.float32, least / len(shards), high / len(shards))
        gain = gain * jnp.repeat(jnp.exp(heights), shape[dim] // blocks).reshape((-1,) + (1,) * (len(shape) - 1 - dim))
    return gain


def scatter_about(rng, extent, width, bound, pieces=(), held_as=jnp.bfloat16):
    drawn = width * jax.random.normal(rng, extent, jnp.float32)
    if pieces:
        drawn = drawn * level_of(rng, extent, pieces, -0.22, 0.18)
    return jnp.clip(drawn, -bound, bound).astype(held_as)


def setup_inputs(seed: int = 0) -> dict:
    key_of = jax.random.split(jax.random.key(seed), 14)
    return {
        "input_tokens": scatter_about(key_of[0], (SAMPLES, TOKENS, D), 1.0, 6.0, ((0, 16),)),
        "output_cotangent": scatter_about(key_of[1], (SAMPLES, TOKENS, D), 2.5, 15.0, ((0, 16),)),
        "query_weight": scatter_about(key_of[2], (D, D), D ** -0.5, 0.21875, ((1, 16),)),
        "key_weight": scatter_about(key_of[3], (D, D), D ** -0.5, 0.21875, ((1, 16),)),
        "value_weight": scatter_about(key_of[4], (D, D), D ** -0.5, 0.21875, ((1, 16),)),
        "output_weight": scatter_about(key_of[5], (D, D), D ** -0.5, 0.21875, ((0, 16),)),
        "pair_bias": draw_pair_bias(jax.random.fold_in(key_of[13], 71), 0),
        "valid_len": jax.random.randint(key_of[7], (1,), TOKENS // 2, TOKENS + 1).astype(jnp.int32),
        "pair_in": scatter_about(key_of[8], (TOKENS, TOKENS, CZ), 1.0, 6.0, ((0, 16), (1, 16))),
        "w_bias": scatter_about(key_of[9], (CZ, HEADS), 1.0, 6.0),
        "t_gate": scatter_about(key_of[10], (LAYERS, CZ, FF), CZ ** -0.5, 0.5),
        "t_up": scatter_about(key_of[11], (LAYERS, CZ, FF), CZ ** -0.5, 0.5),
        "t_down": scatter_about(key_of[12], (LAYERS, FF, CZ), FF ** -0.5, 0.375),
    }


EPS_NORM = 1e-05
MASKED = -1e+30

def layer_forward(field, gate_weight, up_weight, down_weight):
    centred = field - lax.optimization_barrier(jnp.mean(field, axis=-1, keepdims=True))
    variance = lax.optimization_barrier(jnp.mean(centred * centred, axis=-1, keepdims=True))
    inv_std = lax.rsqrt(variance + EPS_NORM)
    normed = centred * inv_std
    normed_low = normed.astype(jnp.bfloat16)
    gate_proj = jnp.dot(normed_low, gate_weight, preferred_element_type=jnp.float32)
    up_proj = jnp.dot(normed_low, up_weight, preferred_element_type=jnp.float32)
    sigmoid_gate = jax.nn.sigmoid(gate_proj)
    hidden = (gate_proj * sigmoid_gate * up_proj).astype(jnp.bfloat16)
    result = field + jnp.dot(hidden, down_weight, preferred_element_type=jnp.float32)
    return (result, (normed, normed_low, inv_std, gate_proj, up_proj, sigmoid_gate, hidden))

def layer_backward(grad_next, saved, gate_weight, up_weight, down_weight):
    normed, normed_low, inv_std, gate_proj, up_proj, sigmoid_gate, hidden = saved
    grad_low = grad_next.astype(jnp.bfloat16)
    down_sum = jnp.dot(hidden.T, grad_low, preferred_element_type=jnp.float32)
    grad_hidden = jnp.dot(grad_low, down_weight.T, preferred_element_type=jnp.float32)
    grad_gate = (grad_hidden * up_proj * sigmoid_gate * (1.0 + gate_proj * (1.0 - sigmoid_gate))).astype(jnp.bfloat16)
    grad_up = (grad_hidden * gate_proj * sigmoid_gate).astype(jnp.bfloat16)
    gate_sum = jnp.dot(normed_low.T, grad_gate, preferred_element_type=jnp.float32)
    up_sum = jnp.dot(normed_low.T, grad_up, preferred_element_type=jnp.float32)
    grad_normed = jnp.dot(grad_gate, gate_weight.T, preferred_element_type=jnp.float32) + jnp.dot(grad_up, up_weight.T, preferred_element_type=jnp.float32)
    inner = inv_std * (grad_normed - lax.optimization_barrier(jnp.mean(grad_normed, axis=-1, keepdims=True)) - normed * lax.optimization_barrier(jnp.mean(grad_normed * normed, axis=-1, keepdims=True)))
    return (grad_next + inner, gate_sum, up_sum, down_sum)

def pair_block(pair_low, grad_top, t_gate, t_up, t_down):
    field = pair_low.astype(jnp.float32)
    saved_list = []
    for layer in range(t_gate.shape[0]):
        field, saved = layer_forward(field, t_gate[layer], t_up[layer], t_down[layer])
        saved_list.append(saved)
    grad_field = grad_top
    gate_list, up_list, down_list = ([], [], [])
    for layer in reversed(range(t_gate.shape[0])):
        grad_field, gate_sum, up_sum, down_sum = layer_backward(grad_field, saved_list[layer], t_gate[layer], t_up[layer], t_down[layer])
        gate_list.insert(0, gate_sum)
        up_list.insert(0, up_sum)
        down_list.insert(0, down_sum)
    return (grad_field, jnp.stack(gate_list), jnp.stack(up_list), jnp.stack(down_list))

def attend(query, keys, values, grad_out, bias_block, kept_keys):
    score_scale = 1.0 / math.sqrt(HD)
    query_f = query.astype(jnp.float32)
    keys_f = keys.astype(jnp.float32)
    values_f = values.astype(jnp.float32)
    grad_f = grad_out.astype(jnp.float32)
    scores = jnp.einsum('sie,sje->sij', query_f, keys_f) * score_scale + bias_block.astype(jnp.float32)[None]
    scores = jnp.where(kept_keys[None, None, :], scores, MASKED)
    row_max = lax.optimization_barrier(jnp.max(scores, axis=-1, keepdims=True))
    exp_scores = jnp.exp(scores - row_max)
    attn_probs = exp_scores / lax.optimization_barrier(jnp.sum(exp_scores, axis=-1, keepdims=True))
    probs_low = attn_probs.astype(jnp.bfloat16)
    grad_probs = jnp.einsum('sie,sje->sij', grad_f, values_f)
    grad_scores = attn_probs * (grad_probs - lax.optimization_barrier(jnp.sum(attn_probs * grad_probs, axis=-1, keepdims=True)))
    scores_low = grad_scores.astype(jnp.bfloat16).astype(jnp.float32)
    value_partial_gradient = lax.optimization_barrier(jnp.sum(grad_scores, axis=0))
    grad_query = (jnp.einsum('sij,sje->sie', scores_low, keys_f) * score_scale).astype(jnp.bfloat16)
    grad_key = (jnp.einsum('sij,sie->sje', scores_low, query_f) * score_scale).astype(jnp.bfloat16)
    grad_value = jnp.einsum('sij,sie->sje', probs_low.astype(jnp.float32), grad_f).astype(jnp.bfloat16)
    return (grad_query, grad_key, grad_value, value_partial_gradient)

def reference(input_tokens, output_cotangent, query_weight, key_weight, value_weight, output_weight, pair_bias, valid_len, pair_in, w_bias, t_gate, t_up, t_down):
    kept_keys = jnp.arange(TOKENS, dtype=jnp.int32) < valid_len[0]
    groups = SAMPLES // SAMP_DEV
    per_group = HEADS // N_HEAD
    tokens_wide_float = input_tokens.astype(jnp.float32)
    query_every_sample = jnp.einsum('tvz,zl->tvl', tokens_wide_float, query_weight.astype(jnp.float32)).astype(jnp.bfloat16)
    key_every_sample = jnp.einsum('tvz,zl->tvl', tokens_wide_float, key_weight.astype(jnp.float32)).astype(jnp.bfloat16)
    value_every_sample = jnp.einsum('tvz,zl->tvl', tokens_wide_float, value_weight.astype(jnp.float32)).astype(jnp.bfloat16)
    attention_every_sample = jnp.einsum('cjy,hy->cjh', output_cotangent.astype(jnp.float32), output_weight.astype(jnp.float32)).astype(jnp.bfloat16)

    def head_fn(head_idx):
        start = head_idx * HD

        def pick_head(array):
            return lax.dynamic_slice_in_dim(array, start, HD, 2).reshape(groups, SAMP_DEV, TOKENS, HD)
        bias_block = lax.dynamic_index_in_dim(pair_bias, head_idx, 0, keepdims=False)

        def group_fn(inputs):
            grad_query, grad_key, grad_value, value_partial_gradient = attend(inputs[0], inputs[1], inputs[2], inputs[3], bias_block, kept_keys)
            return (grad_query, grad_key, grad_value, value_partial_gradient.astype(jnp.bfloat16))
        head_outs = lax.map(group_fn, (pick_head(query_every_sample), pick_head(key_every_sample), pick_head(value_every_sample), pick_head(attention_every_sample)))
        bias_sum = lax.optimization_barrier(jnp.sum(lax.optimization_barrier(head_outs[3]).astype(jnp.float32), axis=0)).astype(jnp.bfloat16)
        return (head_outs[0].reshape(SAMPLES, TOKENS, HD), head_outs[1].reshape(SAMPLES, TOKENS, HD), head_outs[2].reshape(SAMPLES, TOKENS, HD), bias_sum)
    grad_query, grad_key, grad_value, d_bias = lax.map(head_fn, jnp.arange(HEADS, dtype=jnp.int32))

    def token_step(running, group_idx):
        first = group_idx * per_group

        def gather_group(array):
            picked = lax.dynamic_slice_in_dim(array, first, per_group, 0)
            return picked.transpose(1, 2, 0, 3).reshape(SAMPLES, TOKENS, per_group * HD)

        def weight_group(weight):
            return lax.dynamic_slice_in_dim(weight, first * HD, per_group * HD, 1)
        joined_gradients = jnp.concatenate([gather_group(grad_query), gather_group(grad_key), gather_group(grad_value)], axis=2).astype(jnp.float32)
        joined_weights = jnp.concatenate([weight_group(query_weight), weight_group(key_weight), weight_group(value_weight)], axis=1).astype(jnp.float32)
        value_partial_gradient = jnp.einsum('tla,ua->tlu', joined_gradients, joined_weights)
        rounded = lax.optimization_barrier(value_partial_gradient.astype(jnp.bfloat16)).astype(jnp.float32)
        return (running + rounded, None)
    running, _ = lax.scan(token_step, jnp.zeros((SAMPLES, TOKENS, D), jnp.float32), jnp.arange(N_HEAD, dtype=jnp.int32))
    d_tokens = running.astype(jnp.bfloat16)
    block_rows = TOKENS // N_HEAD

    def pair_step(carry, block_idx):
        start = block_idx * block_rows
        pair_rows = lax.dynamic_slice_in_dim(pair_in, start, block_rows, 0)
        bias_rows = lax.dynamic_slice_in_dim(d_bias, start, block_rows, 1)
        grad_top = jnp.einsum('hrc,zh->rcz', bias_rows.astype(jnp.float32), w_bias.astype(jnp.float32))
        grad_field, gate_sum, up_sum, down_sum = pair_block(pair_rows.reshape(block_rows * TOKENS, CZ), grad_top.reshape(block_rows * TOKENS, CZ), t_gate, t_up, t_down)
        new_carry = (carry[0] + gate_sum, carry[1] + up_sum, carry[2] + down_sum)
        return (new_carry, grad_field.reshape(block_rows, TOKENS, CZ).astype(jnp.bfloat16))
    init = (jnp.zeros(t_gate.shape, jnp.float32), jnp.zeros(t_up.shape, jnp.float32), jnp.zeros(t_down.shape, jnp.float32))
    sums, pair_blocks = lax.scan(pair_step, init, jnp.arange(N_HEAD, dtype=jnp.int32))
    d_pair = pair_blocks.reshape(TOKENS, TOKENS, CZ)
    return (d_tokens, d_pair, sums[0] / TOKENS, sums[1] / TOKENS, sums[2] / TOKENS)
```

```python
import math

import jax
import jax.numpy as jnp
from jax import lax
from jax.sharding import Mesh
from jax.sharding import PartitionSpec as P

HD = 48
SAMP = ("yh", "x", "core")
HEAD = ("yl", "z")
PLANE = ("yh", "x", "yl")


EPS_NORM = 1e-05
MASKED = -1e30


def sum_in_order(pieces, axes, turns):
    inside = pieces.shape[1:]
    pieces = pieces.reshape(*(lax.axis_size(a) for a in axes), *inside)
    pieces = jnp.moveaxis(pieces, turns, range(len(axes))).reshape(-1, *inside)
    for k in turns:
        pieces = lax.psum_scatter(pieces, axes[k], scatter_dimension=0, tiled=True)
    return pieces[0]


def cut_along(array, dim, length):
    dims = array.shape
    pieces = array.reshape(*dims[:dim], length, dims[dim] // length, *dims[dim + 1 :])
    return jnp.moveaxis(pieces, dim, 0)


def scatter_axes(array, axes, turns, dim):
    length = lax.axis_size(axes)
    return sum_in_order(cut_along(array, dim, length), axes, turns)


def sent_and_summed(array, axis, dim):
    length = lax.axis_size(axis)
    pieces = lax.all_to_all(cut_along(array, dim, length), axis, 0, 0, tiled=True)
    return jnp.sum(pieces.astype(jnp.float32), axis=0)


def exchange(pieces, axes):
    return lax.all_to_all(pieces, axes, 0, 0, tiled=True)


def summed(pieces):
    return jnp.sum(pieces.astype(jnp.float32), axis=0)


def other_core(array):
    return lax.ppermute(array, "core", [(0, 1), (1, 0)])


def sum_everywhere(arrays):
    low = jnp.concatenate([a.astype(jnp.bfloat16).reshape(-1) for a in arrays])
    halves = low.reshape(2, 16, -1, 128)
    second = lax.axis_index("core") == 1
    kept = jnp.where(second, halves[1], halves[0])
    sent = jnp.where(second, halves[0], halves[1])
    half = (kept.astype(jnp.float32) + other_core(sent).astype(jnp.float32)).astype(jnp.bfloat16)
    block = summed(exchange(half, PLANE)).astype(jnp.bfloat16)
    block = summed(exchange(jnp.broadcast_to(block, (8, *block.shape)), "z")).astype(jnp.bfloat16)
    half = exchange(jnp.broadcast_to(block, (16, *block.shape)), PLANE)
    other = other_core(half)
    total = jnp.concatenate([jnp.where(second, other, half), jnp.where(second, half, other)])
    total = total.astype(jnp.float32).reshape(-1)
    gathered, at = [], 0
    for a in arrays:
        gathered.append(total[at : at + a.size].reshape(a.shape))
        at += a.size
    return tuple(gathered)


def layer_forward(field, gate_weight, up_weight, down_weight):
    centred = field - jnp.mean(field, axis=-1, keepdims=True)
    variance = jnp.mean(centred * centred, axis=-1, keepdims=True)
    inv_std = lax.rsqrt(variance + EPS_NORM)
    normed = centred * inv_std
    normed_low = normed.astype(jnp.bfloat16)
    gate_proj = jnp.dot(normed_low, gate_weight, preferred_element_type=jnp.float32)
    up_proj = jnp.dot(normed_low, up_weight, preferred_element_type=jnp.float32)
    sigmoid_gate = jax.nn.sigmoid(gate_proj)
    hidden = (gate_proj * sigmoid_gate * up_proj).astype(jnp.bfloat16)
    result = field + jnp.dot(hidden, down_weight, preferred_element_type=jnp.float32)
    return (result, (normed, normed_low, inv_std, gate_proj, up_proj, sigmoid_gate, hidden))


def layer_backward(grad_next, saved, gate_weight, up_weight, down_weight):
    normed, normed_low, inv_std, gate_proj, up_proj, sigmoid_gate, hidden = saved
    grad_low = grad_next.astype(jnp.bfloat16)
    down_sum = jnp.dot(hidden.T, grad_low, preferred_element_type=jnp.float32)
    grad_hidden = jnp.dot(grad_low, down_weight.T, preferred_element_type=jnp.float32)
    grad_gate = (
        grad_hidden * up_proj * sigmoid_gate * (1.0 + gate_proj * (1.0 - sigmoid_gate))
    ).astype(jnp.bfloat16)
    grad_up = (grad_hidden * gate_proj * sigmoid_gate).astype(jnp.bfloat16)
    gate_sum = jnp.dot(normed_low.T, grad_gate, preferred_element_type=jnp.float32)
    up_sum = jnp.dot(normed_low.T, grad_up, preferred_element_type=jnp.float32)
    grad_normed = jnp.dot(grad_gate, gate_weight.T, preferred_element_type=jnp.float32) + jnp.dot(
        grad_up, up_weight.T, preferred_element_type=jnp.float32
    )
    inner = inv_std * (
        grad_normed
        - jnp.mean(grad_normed, axis=-1, keepdims=True)
        - normed * jnp.mean(grad_normed * normed, axis=-1, keepdims=True)
    )
    return (grad_next + inner, gate_sum, up_sum, down_sum)


def pair_block(pair_low, grad_top, t_gate, t_up, t_down):
    field = pair_low.astype(jnp.float32)
    saved_list = []
    for layer in range(t_gate.shape[0]):
        field, saved = layer_forward(field, t_gate[layer], t_up[layer], t_down[layer])
        saved_list.append(saved)
    grad_field = grad_top
    gate_list, up_list, down_list = ([], [], [])
    for layer in reversed(range(t_gate.shape[0])):
        grad_field, gate_sum, up_sum, down_sum = layer_backward(
            grad_field, saved_list[layer], t_gate[layer], t_up[layer], t_down[layer]
        )
        gate_list.insert(0, gate_sum)
        up_list.insert(0, up_sum)
        down_list.insert(0, down_sum)
    return (grad_field, jnp.stack(gate_list), jnp.stack(up_list), jnp.stack(down_list))


def per_device(
    input_tokens,
    output_cotangent,
    query_weight,
    key_weight,
    value_weight,
    output_weight,
    pair_bias,
    valid_len,
    pair_in,
    w_bias,
    t_gate,
    t_up,
    t_down,
):
    samples = input_tokens.shape[0]
    tokens = input_tokens.shape[1]
    local_width = query_weight.shape[1]
    local_heads = local_width // HD
    score_scale = 1.0 / math.sqrt(HD)
    kept_keys = jnp.arange(tokens, dtype=jnp.int32) < valid_len[0]
    inner_weight = jnp.concatenate([query_weight, key_weight, value_weight], axis=1)
    projected = jnp.einsum(
        "tvz,zl->tvl", input_tokens, inner_weight, preferred_element_type=jnp.float32
    ).astype(jnp.bfloat16)
    attention_gradient = jnp.einsum(
        "cjy,hy->cjh", output_cotangent, output_weight, preferred_element_type=jnp.float32
    ).astype(jnp.bfloat16)
    split_heads = projected.reshape(samples, tokens, 3, local_heads, HD).transpose(2, 3, 0, 1, 4)
    attn_heads = attention_gradient.reshape(samples, tokens, local_heads, HD).transpose(2, 0, 1, 3)

    def attend_head(inputs):
        query, keys, values, grad_out, bias_block = inputs
        scores = (
            jnp.einsum("sie,sje->sij", query, keys, preferred_element_type=jnp.float32)
            * score_scale
            + bias_block.astype(jnp.float32)[None]
        )
        scores = jnp.where(kept_keys[None, None, :], scores, MASKED)
        row_max = jnp.max(scores, axis=-1, keepdims=True)
        exp_scores = jnp.exp(scores - row_max)
        attn_probs = exp_scores / jnp.sum(exp_scores, axis=-1, keepdims=True)
        probs_low = attn_probs.astype(jnp.bfloat16)
        grad_probs = jnp.einsum(
            "sie,sje->sij", grad_out, values, preferred_element_type=jnp.float32
        )
        grad_scores = attn_probs * (
            grad_probs - jnp.sum(attn_probs * grad_probs, axis=-1, keepdims=True)
        )
        scores_low = grad_scores.astype(jnp.bfloat16)
        value_partial_gradient = jnp.sum(grad_scores, axis=0)
        grad_query = (
            jnp.einsum("sij,sje->sie", scores_low, keys, preferred_element_type=jnp.float32)
            * score_scale
        ).astype(jnp.bfloat16)
        grad_key = (
            jnp.einsum("sij,sie->sje", scores_low, query, preferred_element_type=jnp.float32)
            * score_scale
        ).astype(jnp.bfloat16)
        grad_value = jnp.einsum(
            "sij,sie->sje", probs_low, grad_out, preferred_element_type=jnp.float32
        ).astype(jnp.bfloat16)
        return (grad_query, grad_key, grad_value, value_partial_gradient)

    head_outs = lax.map(
        attend_head, (split_heads[0], split_heads[1], split_heads[2], attn_heads, pair_bias)
    )
    joined_gradients = jnp.concatenate(
        [
            part_grad.transpose(1, 2, 0, 3).reshape(samples, tokens, local_width)
            for part_grad in head_outs[:3]
        ],
        axis=2,
    )
    token_terms = jnp.einsum(
        "tla,ua->tlu", joined_gradients, inner_weight, preferred_element_type=jnp.float32
    ).astype(jnp.bfloat16)
    d_tokens = scatter_axes(token_terms, HEAD, (1, 0), 2).astype(jnp.float32).astype(jnp.bfloat16)
    bias_parts = head_outs[3].astype(jnp.bfloat16)
    summed = sent_and_summed(bias_parts, SAMP, 2)
    owned_grad = lax.all_to_all(
        summed.astype(jnp.bfloat16), HEAD, split_axis=1, concat_axis=0, tiled=True
    )
    pair_rows, pair_cols, channels = pair_in.shape
    grad_top = jnp.einsum("hrc,zh->rcz", owned_grad, w_bias, preferred_element_type=jnp.float32)
    grad_field, gate_sum, up_sum, down_sum = pair_block(
        pair_in.reshape(pair_rows * pair_cols, channels),
        grad_top.reshape(pair_rows * pair_cols, channels),
        t_gate,
        t_up,
        t_down,
    )
    total_gate, total_up, total_down = sum_everywhere(
        (gate_sum / tokens, up_sum / tokens, down_sum / tokens)
    )
    d_pair = grad_field.reshape(pair_rows, pair_cols, channels).astype(jnp.bfloat16)
    return (d_tokens, d_pair, total_gate, total_up, total_down)


def solution(mesh):
    torus = Mesh(mesh.devices.reshape(2, 4, 2, 2, 8), ("yh", "x", "core", "yl", "z"))
    return jax.shard_map(
        per_device,
        mesh=torus,
        in_specs=(
            P(SAMP, None, None),
            P(SAMP, None, None),
            P(None, HEAD),
            P(None, HEAD),
            P(None, HEAD),
            P(HEAD, None),
            P(HEAD, None, None),
            P(),
            P(HEAD, SAMP, None),
            P(),
            P(),
            P(),
            P(),
        ),
        out_specs=(P(SAMP, None, HEAD), P(HEAD, SAMP, None), P(), P(), P()),
        check_vma=False,
    )
```

```python
import math

import jax
import jax.numpy as jnp
from jax import lax
from jax.experimental import pallas as pl
from jax.experimental.pallas import tpu as pltpu
from jax.sharding import Mesh
from jax.sharding import PartitionSpec as P


HD = 48
SAMP = ("yh", "x", "core")
HEAD = ("yl", "z")
PLANE = ("yh", "x", "yl")
LANES = 128


EPS_NORM = 1e-05
MASKED = -1e30
LOW = jnp.bfloat16
WIDE = jnp.float32
VMEM = pl.BlockSpec(memory_space=pltpu.VMEM)
SMEM = pl.BlockSpec(memory_space=pltpu.SMEM)


def room(mib):
    return pltpu.CompilerParams(vmem_limit_bytes=mib << 20)


def nn(a, b):
    return lax.dot_general(a, b, (((1,), (0,)), ((), ())), preferred_element_type=WIDE)


def nt(a, b):
    return lax.dot_general(a, b, (((1,), (1,)), ((), ())), preferred_element_type=WIDE)


def tn(a, b):
    return lax.dot_general(a, b, (((0,), (0,)), ((), ())), preferred_element_type=WIDE)


def like(shape, dtype):
    return jax.ShapeDtypeStruct(shape, dtype)


def attend_kernel(
    valid, tokens, cotangent, wq, wk, wv, wo, bias, part, dscores, probs, queries, keys, grads
):
    samples, length, _ = tokens.shape
    scale = 1.0 / math.sqrt(HD)
    key_rows, value_rows = [], []
    for s in range(samples):
        x = tokens[s]
        queries[s] = nt(wq[...], x).astype(LOW)
        keys[s] = nt(wk[...], x).astype(LOW)
        grads[s] = nt(wo[...], cotangent[s]).astype(LOW)
        key_rows.append(nt(x, wk[...]).astype(LOW))
        value_rows.append(nt(x, wv[...]).astype(LOW))
    kept = lax.broadcasted_iota(jnp.int32, (length, LANES), 0) < valid[0]
    for at in range(0, length, LANES):
        block = slice(at, at + LANES)
        turned = jnp.where(kept, bias[block, :].astype(WIDE).T, MASKED)
        total = None
        for s in range(samples):
            scores = nn(key_rows[s], queries[s, :, block]) * scale + turned
            exps = jnp.exp(scores - jnp.max(scores, axis=0, keepdims=True))
            prob = exps * (1.0 / jnp.sum(exps, axis=0, keepdims=True))
            probs[s, :, block] = prob.astype(LOW)
            grad_prob = nn(value_rows[s], grads[s, :, block])
            mean = jnp.sum(prob * grad_prob, axis=0, keepdims=True)
            dscore = prob * (grad_prob - mean)
            dscores[s, :, block] = dscore.astype(LOW)
            total = dscore if total is None else total + dscore
        part[:, block] = total.astype(LOW)


def attend(valid, tokens, cotangent, wq, wk, wv, wo, bias):
    samples, length, _ = tokens.shape
    square = like((samples, length, length), LOW)
    heads = like((samples, HD, length), LOW)
    return pl.pallas_call(
        attend_kernel,
        out_shape=(like((length, length), LOW), square, square, heads, heads, heads),
        in_specs=[SMEM] + [VMEM] * 7,
        out_specs=[VMEM] * 6,
        compiler_params=room(16),
        name="attend",
    )(valid, tokens, cotangent, wq, wk, wv, wo, bias)


def token_kernel(place, dscores, probs, queries, keys, grads, wq, wk, wv, kept, sent):
    scale = 1.0 / math.sqrt(HD)
    weight = jnp.concatenate([wq[...], wk[...], wv[...]], axis=0)
    for s in range(dscores.shape[0]):
        d = dscores[s]
        joined = jnp.concatenate(
            [
                (nn(keys[s], d) * scale).astype(LOW),
                (nt(queries[s], d) * scale).astype(LOW),
                nt(grads[s], probs[s]).astype(LOW),
            ],
            axis=0,
        )
        terms = tn(weight, joined).astype(LOW)
        for r in range(16):
            z = r % 8
            slot = (z % 2 * 4 + z // 2 % 2 * 2 + z // 4) ^ place[1]
            piece = terms[r * HD : (r + 1) * HD]

            @pl.when(place[0] == r // 8)
            def _(slot=slot, piece=piece):
                kept[slot, s] = piece

            @pl.when(place[0] != r // 8)
            def _(slot=slot, piece=piece):
                sent[slot, s] = piece


def token_pieces(place, dscores, probs, queries, keys, grads, wq, wk, wv):
    samples, length, _ = dscores.shape
    half = like((8, samples, HD, length), LOW)
    return pl.pallas_call(
        token_kernel,
        out_shape=(half, half),
        in_specs=[SMEM] + [VMEM] * 8,
        out_specs=[VMEM] * 2,
        compiler_params=room(16),
        name="token_pieces",
    )(place, dscores, probs, queries, keys, grads, wq, wk, wv)


def rows_kernel(pieces, out):
    total = pieces[0].astype(WIDE)
    for k in range(1, pieces.shape[0]):
        total = total + pieces[k].astype(WIDE)
    turned = total.T.reshape(out.shape[0], LANES // total.shape[0], -1, total.shape[0])
    packed = jnp.concatenate([turned[:, q] for q in range(turned.shape[1])], axis=-1)
    out[...] = packed.astype(LOW)


def bias_rows(pieces):
    count, cols, length = pieces.shape
    return pl.pallas_call(
        rows_kernel,
        out_shape=like((count, length // count * cols // LANES, LANES), LOW),
        in_specs=[VMEM],
        out_specs=VMEM,
        compiler_params=room(4),
        name="bias_rows_sum",
    )(pieces)


def forward_kernel(pair, t_gate, t_up, t_down, normed, inv, turned, hidden_t, by_gate, by_up):
    field = pair[...].astype(WIDE)
    for layer in range(t_gate.shape[0]):
        centred = field - jnp.mean(field, axis=-1, keepdims=True)
        variance = jnp.mean(centred * centred, axis=-1, keepdims=True)
        inv_std = lax.rsqrt(variance + EPS_NORM)
        unit = centred * inv_std
        low = unit.astype(LOW)
        gate = nn(low, t_gate[layer])
        up = nn(low, t_up[layer])
        sig = jax.nn.sigmoid(gate)
        act = gate * sig
        hidden = (act * up).astype(LOW)
        normed[layer] = unit
        inv[layer] = jnp.broadcast_to(inv_std, unit.shape)
        turned[layer] = low.T
        hidden_t[layer] = hidden.T
        by_gate[layer] = up * (sig * (1.0 + gate * (1.0 - sig)))
        by_up[layer] = act
        if layer + 1 < t_gate.shape[0]:
            field = field + nn(hidden, t_down[layer])


def forward(pair, t_gate, t_up, t_down):
    pairs, channels = pair.shape
    layers, _, width = t_gate.shape
    return pl.pallas_call(
        forward_kernel,
        out_shape=(
            like((layers, pairs, channels), WIDE),
            like((layers, pairs, channels), WIDE),
            like((layers, channels, pairs), LOW),
            like((layers, width, pairs), LOW),
            like((layers, pairs, width), WIDE),
            like((layers, pairs, width), WIDE),
        ),
        in_specs=[VMEM] * 4,
        out_specs=[VMEM] * 6,
        compiler_params=room(20),
        name="pair_forward",
    )(pair, t_gate, t_up, t_down)


def backward_kernel(
    core, packed, spread, normed, inv, turned, hidden_t, by_gate, by_up, t_gate, t_up, t_down,
    d_pair, kept, sent, wide_rows, grad_top,
):
    heads = packed.shape[0]
    channels = normed.shape[2]
    rows = cols = math.isqrt(normed.shape[1])
    group = packed.shape[1]
    for q in range(LANES // cols):
        piece = packed[:, :, q * cols : (q + 1) * cols].astype(WIDE)
        for h in range(heads):
            wide_rows[h * rows + q * group : h * rows + (q + 1) * group, 0:cols] = piece[h]
    per_dot = LANES // heads
    for block in range(rows // per_dot):
        picked = jnp.concatenate(
            [
                wide_rows[pl.ds(block * per_dot + i, heads, stride=rows), :]
                for i in range(per_dot)
            ],
            axis=0,
        )
        top = nn(picked.T[0:cols].astype(LOW), spread[...])
        for i in range(per_dot):
            first = (block * per_dot + i) * cols
            grad_top[first : first + cols, :] = top[:, i * channels : (i + 1) * channels]
    grad = grad_top[...]
    share = 1.0 / (heads * rows)
    for layer in reversed(range(normed.shape[0])):
        low = grad.astype(LOW)
        down_sum = nn(hidden_t[layer], low)
        grad_hidden = nt(low, t_down[layer])
        grad_gate = (grad_hidden * by_gate[layer]).astype(LOW)
        grad_up = (grad_hidden * by_up[layer]).astype(LOW)
        gate_sum = nn(turned[layer], grad_gate)
        up_sum = nn(turned[layer], grad_up)
        for m, weight_sum in enumerate((gate_sum, up_sum, down_sum)):
            if weight_sum.shape[1] != LANES:
                weight_sum = jnp.concatenate(
                    [weight_sum[:, :LANES], weight_sum[:, LANES:]], axis=0
                )
            weight_sum = (weight_sum * share).astype(LOW).reshape(16, 16, LANES)

            @pl.when(core[0] == layer)
            def _(m=m, weight_sum=weight_sum):
                kept[:, m] = weight_sum

            @pl.when(core[0] != layer)
            def _(m=m, weight_sum=weight_sum):
                sent[:, m] = weight_sum

        grad_normed = nt(grad_gate, t_gate[layer]) + nt(grad_up, t_up[layer])
        unit = normed[layer]
        grad = grad + inv[layer] * (
            grad_normed
            - jnp.mean(grad_normed, axis=-1, keepdims=True)
            - unit * jnp.mean(grad_normed * unit, axis=-1, keepdims=True)
        )
    d_pair[...] = grad.astype(LOW)


def backward(core, grad_rows, spread, saved, t_gate, t_up, t_down):
    pairs, channels = saved[0].shape[1:]
    heads, rows = grad_rows.shape[0], math.isqrt(pairs)
    half = like((16, 3, 16, LANES), LOW)
    return pl.pallas_call(
        backward_kernel,
        out_shape=(like((pairs, channels), LOW), half, half),
        in_specs=[SMEM] + [VMEM] * 11,
        out_specs=[VMEM] * 3,
        scratch_shapes=[
            pltpu.VMEM((heads * rows, LANES), WIDE),
            pltpu.VMEM((pairs, channels), WIDE),
        ],
        compiler_params=room(20),
        name="pair_backward",
    )(core, grad_rows, spread, *saved, t_gate, t_up, t_down)


def exchange(pieces, axes):
    return lax.all_to_all(pieces, axes, 0, 0, tiled=True)


def summed(pieces):
    return jnp.sum(pieces.astype(WIDE), axis=0).astype(LOW)


def flipped(array, axis, bit):
    return lax.ppermute(array, axis, [(k, k ^ bit) for k in range(lax.axis_size(axis))])


def added(kept, received):
    return (kept.astype(WIDE) + received.astype(WIDE)).astype(LOW)


def copies(block, count):
    return jnp.broadcast_to(block, (count, *block.shape))


def sum_everywhere(kept, sent):
    half = added(kept, flipped(sent, "core", 1))
    block = summed(exchange(half, PLANE))
    block = summed(exchange(copies(block, 8), "z"))
    half = exchange(copies(block, 16), PLANE)
    other = flipped(half, "core", 1)
    second = lax.axis_index("core") == 1
    layers = jnp.stack([jnp.where(second, other, half), jnp.where(second, half, other)])
    layers = layers.astype(WIDE).reshape(2, 16, 3, 16, LANES)
    gate, up, down = (layers[:, :, m].reshape(2, 256, LANES) for m in range(3))

    def wide(a):
        return a.reshape(2, 2, 128, LANES).transpose(0, 2, 1, 3).reshape(2, 128, 256)

    return wide(gate), wide(up), down


def token_sum(kept, sent):
    piece = added(kept, flipped(sent, "yl", 1))
    for bit in (1, 2, 4):
        count = piece.shape[0] // 2
        piece = added(piece[:count], flipped(piece[count:], "z", bit))
    return piece[0]


def per_device(
    input_tokens,
    output_cotangent,
    query_weight,
    key_weight,
    value_weight,
    output_weight,
    pair_bias,
    valid_len,
    pair_in,
    w_bias,
    t_gate,
    t_up,
    t_down,
):
    tokens = input_tokens.shape[1]
    rows, cols, channels = pair_in.shape
    heads = w_bias.shape[1]
    wq, wk, wv = query_weight.T, key_weight.T, value_weight.T
    core = lax.axis_index("core").reshape(1)
    z = lax.axis_index("z")
    place = jnp.stack([lax.axis_index("yl"), z % 2 * 4 + z // 2 % 2 * 2 + z // 4])
    part, dscores, probs, queries, keys, grads = attend(
        valid_len, input_tokens, output_cotangent, wq, wk, wv, output_weight, pair_bias[0]
    )
    received = exchange(part.reshape(16, tokens // 16, tokens), SAMP)
    kept, sent = token_pieces(place, dscores, probs, queries, keys, grads, wq, wk, wv)
    saved = forward(pair_in.reshape(rows * cols, channels), t_gate, t_up, t_down)
    per_dot = LANES // heads
    spread = jnp.einsum("ij,ch->ihjc", jnp.eye(per_dot, dtype=LOW), w_bias)
    spread = spread.reshape(LANES, per_dot * channels)
    grad_rows = exchange(bias_rows(received), HEAD)
    d_tokens = token_sum(kept, sent)
    d_pair, own, other = backward(core, grad_rows, spread, saved, t_gate, t_up, t_down)
    d_gate, d_up, d_down = sum_everywhere(own.reshape(16, 48, LANES), other.reshape(16, 48, LANES))
    return (d_tokens.transpose(0, 2, 1), d_pair.reshape(rows, cols, channels), d_gate, d_up, d_down)


def solution(mesh):
    torus = Mesh(mesh.devices.reshape(2, 4, 2, 2, 8), ("yh", "x", "core", "yl", "z"))
    return jax.shard_map(
        per_device,
        mesh=torus,
        in_specs=(
            P(SAMP, None, None),
            P(SAMP, None, None),
            P(None, HEAD),
            P(None, HEAD),
            P(None, HEAD),
            P(HEAD, None),
            P(HEAD, None, None),
            P(),
            P(HEAD, SAMP, None),
            P(),
            P(),
            P(),
            P(),
        ),
        out_specs=(P(SAMP, None, HEAD), P(HEAD, SAMP, None), P(), P(), P()),
        check_vma=False,
    )
```

```python
import math

import jax
import jax.numpy as jnp
from jax import lax
from jax.experimental import pallas as pl
from jax.experimental.pallas import tpu as pltpu
from jax.sharding import Mesh
from jax.sharding import PartitionSpec as P


HD = 48
SAMP = ("yh", "x", "core")
HEAD = ("yl", "z")
PLANE = ("yh", "x", "yl")
LANES = 128


EPS_NORM = 1e-05
MASKED = -1e30
LOW = jnp.bfloat16
WIDE = jnp.float32
VMEM = pl.BlockSpec(memory_space=pltpu.VMEM)
SMEM = pl.BlockSpec(memory_space=pltpu.SMEM)
FAR = pl.BlockSpec(memory_space=pltpu.HBM)


def room(mib):
    return pltpu.CompilerParams(vmem_limit_bytes=mib << 20)


def nn(a, b):
    return lax.dot_general(a, b, (((1,), (0,)), ((), ())), preferred_element_type=WIDE)


def nt(a, b):
    return lax.dot_general(a, b, (((1,), (1,)), ((), ())), preferred_element_type=WIDE)


def tn(a, b):
    return lax.dot_general(a, b, (((0,), (0,)), ((), ())), preferred_element_type=WIDE)


def like(shape, dtype):
    return jax.ShapeDtypeStruct(shape, dtype)


def far_away(*arrays):
    return [pltpu.with_memory_space_constraint(a, pltpu.HBM) for a in arrays]


def started(pairs, sems):
    moves = [pltpu.make_async_copy(a, b, sems.at[k]) for k, (a, b) in enumerate(pairs)]
    for move in moves:
        move.start()
    return moves


def waited(moves):
    for move in moves:
        move.wait()


def attend_kernel(
    valid, tokens_far, cotangent_far, wq_far, wk_far, wv_far, wo_far, bias_far,
    part_far, dscores, probs, queries_far, keys_far, grads_far,
    tokens, cotangent, wq, wk, wv, wo, bias, part, queries, keys, grads, sems, out_sems,
):
    samples, length, _ = tokens.shape
    scale = 1.0 / math.sqrt(HD)
    moves = started(
        [
            (wq_far, wq),
            (wk_far, wk),
            (wv_far, wv),
            (tokens_far.at[0], tokens.at[0]),
            (wo_far, wo),
            (cotangent_far.at[0], cotangent.at[0]),
            (tokens_far.at[1], tokens.at[1]),
            (cotangent_far.at[1], cotangent.at[1]),
            (bias_far, bias),
        ],
        sems,
    )
    key_rows, value_rows = [], []
    for s in range(samples):
        waited(moves[:6] if s == 0 else moves[6:8])
        x = tokens[s]
        queries[s] = nt(wq[...], x).astype(LOW)
        keys[s] = nt(wk[...], x).astype(LOW)
        grads[s] = nt(wo[...], cotangent[s]).astype(LOW)
        key_rows.append(nt(x, wk[...]).astype(LOW))
        value_rows.append(nt(x, wv[...]).astype(LOW))
    leaving = started(
        [(queries, queries_far), (keys, keys_far), (grads, grads_far)], out_sems.at[0]
    )
    waited(moves[8:])
    kept = lax.broadcasted_iota(jnp.int32, (length, LANES), 0) < valid[0]
    for at in range(0, length, LANES):
        block = slice(at, at + LANES)
        turned = jnp.where(kept, bias[block, :].astype(WIDE).T, MASKED)
        total = None
        for s in range(samples):
            scores = nn(key_rows[s], queries[s, :, block]) * scale + turned
            exps = jnp.exp(scores - jnp.max(scores, axis=0, keepdims=True))
            prob = exps * (1.0 / jnp.sum(exps, axis=0, keepdims=True))
            probs[s, :, block] = prob.astype(LOW)
            grad_prob = nn(value_rows[s], grads[s, :, block])
            mean = jnp.sum(prob * grad_prob, axis=0, keepdims=True)
            dscore = prob * (grad_prob - mean)
            dscores[s, :, block] = dscore.astype(LOW)
            total = dscore if total is None else total + dscore
        part[:, block] = total.astype(LOW)
        leaving += started([(part.at[:, block], part_far.at[:, block])], out_sems.at[1, at // LANES :])
    waited(leaving)


def attend(valid, tokens, cotangent, wq, wk, wv, wo, bias):
    samples, length, _ = tokens.shape
    square = like((samples, length, length), LOW)
    heads = pltpu.HBM((samples, HD, length), LOW)
    return pl.pallas_call(
        attend_kernel,
        out_shape=(pltpu.HBM((length, length), LOW), square, square, heads, heads, heads),
        in_specs=[SMEM] + [FAR] * 7,
        out_specs=[FAR] + [VMEM] * 2 + [FAR] * 3,
        scratch_shapes=[
            pltpu.VMEM(a.shape, LOW) for a in (tokens, cotangent, wq, wk, wv, wo, bias)
        ]
        + [pltpu.VMEM((length, length), LOW)]
        + [pltpu.VMEM((samples, HD, length), LOW)] * 3
        + [pltpu.SemaphoreType.DMA((9,)), pltpu.SemaphoreType.DMA((2, 4))],
        compiler_params=room(16),
        name="attend",
    )(valid, *far_away(tokens, cotangent, wq, wk, wv, wo, bias))


def token_kernel(place, dscores, probs, *refs):
    far, (kept, sent), near, sems = refs[:6], refs[6:8], refs[8:14], refs[14]
    queries, keys, grads, wq, wk, wv = near
    waited(started(list(zip(far, near)), sems))
    scale = 1.0 / math.sqrt(HD)
    weight = jnp.concatenate([wq[...], wk[...], wv[...]], axis=0)
    for s in range(dscores.shape[0]):
        d = dscores[s]
        joined = jnp.concatenate(
            [
                (nn(keys[s], d) * scale).astype(LOW),
                (nt(queries[s], d) * scale).astype(LOW),
                nt(grads[s], probs[s]).astype(LOW),
            ],
            axis=0,
        )
        terms = tn(weight, joined).astype(LOW)
        for r in range(16):
            z = r % 8
            slot = (z % 2 * 4 + z // 2 % 2 * 2 + z // 4) ^ place[1]
            piece = terms[r * HD : (r + 1) * HD]

            @pl.when(place[0] == r // 8)
            def _(slot=slot, piece=piece):
                kept[slot, s] = piece

            @pl.when(place[0] != r // 8)
            def _(slot=slot, piece=piece):
                sent[slot, s] = piece


def token_pieces(place, dscores, probs, queries, keys, grads, wq, wk, wv):
    samples, length, _ = dscores.shape
    half = like((8, samples, HD, length), LOW)
    return pl.pallas_call(
        token_kernel,
        out_shape=(half, half),
        in_specs=[SMEM] + [VMEM] * 2 + [FAR] * 6,
        out_specs=[VMEM] * 2,
        scratch_shapes=[pltpu.VMEM(a.shape, LOW) for a in (queries, keys, grads, wq, wk, wv)]
        + [pltpu.SemaphoreType.DMA((6,))],
        compiler_params=room(16),
        name="token_pieces",
    )(place, dscores, probs, *far_away(queries, keys, grads, wq, wk, wv))


def rows_kernel(pieces, out):
    total = pieces[0].astype(WIDE)
    for k in range(1, pieces.shape[0]):
        total = total + pieces[k].astype(WIDE)
    turned = total.T.reshape(out.shape[0], LANES // total.shape[0], -1, total.shape[0])
    packed = jnp.concatenate([turned[:, q] for q in range(turned.shape[1])], axis=-1)
    out[...] = packed.astype(LOW)


def bias_rows(pieces):
    count, cols, length = pieces.shape
    return pl.pallas_call(
        rows_kernel,
        out_shape=like((count, length // count * cols // LANES, LANES), LOW),
        in_specs=[VMEM],
        out_specs=VMEM,
        compiler_params=room(4),
        name="bias_rows_sum",
    )(pieces)


def forward_kernel(pair_far, t_gate_far, t_up_far, t_down_far, *refs):
    far, (pair, t_gate, t_up, t_down, *near, in_sems, out_sems) = refs[:6], refs[6:]
    normed, inv, turned, hidden_t, by_gate, by_up = near
    layers = t_gate.shape[0]
    moves = started(
        [(pair_far, pair), (t_gate_far, t_gate), (t_up_far, t_up), (t_down_far, t_down)], in_sems
    )
    waited(moves)
    field = pair[...].astype(WIDE)
    moves = []
    for layer in range(layers):
        centred = field - jnp.mean(field, axis=-1, keepdims=True)
        variance = jnp.mean(centred * centred, axis=-1, keepdims=True)
        inv_std = lax.rsqrt(variance + EPS_NORM)
        unit = centred * inv_std
        low = unit.astype(LOW)
        gate = nn(low, t_gate[layer])
        up = nn(low, t_up[layer])
        sig = jax.nn.sigmoid(gate)
        act = gate * sig
        hidden = (act * up).astype(LOW)
        normed[layer] = unit
        inv[layer] = jnp.broadcast_to(inv_std, unit.shape)
        turned[layer] = low.T
        hidden_t[layer] = hidden.T
        by_gate[layer] = (up * (sig * (1.0 + gate * (1.0 - sig)))).astype(LOW)
        by_up[layer] = act.astype(LOW)
        pairs = [(a.at[layer], b.at[layer]) for a, b in zip(near, far)]
        moves += started(pairs, out_sems.at[layer])
        if layer + 1 < layers:
            field = field + nn(hidden, t_down[layer])
    waited(moves)


def saved_shapes(pairs, channels, layers, width):
    return (
        ((layers, pairs, channels), WIDE),
        ((layers, pairs, channels), WIDE),
        ((layers, channels, pairs), LOW),
        ((layers, width, pairs), LOW),
        ((layers, pairs, width), LOW),
        ((layers, pairs, width), LOW),
    )


def forward(pair, t_gate, t_up, t_down):
    layers, _, width = t_gate.shape
    shapes = saved_shapes(*pair.shape, layers, width)
    return pl.pallas_call(
        forward_kernel,
        out_shape=[pltpu.HBM(*a) for a in shapes],
        in_specs=[FAR] * 4,
        out_specs=[FAR] * 6,
        scratch_shapes=[pltpu.VMEM(a.shape, LOW) for a in (pair, t_gate, t_up, t_down)]
        + [pltpu.VMEM(*a) for a in shapes]
        + [pltpu.SemaphoreType.DMA((4,)), pltpu.SemaphoreType.DMA((layers, 6))],
        compiler_params=room(24),
        name="pair_forward",
    )(*far_away(pair, t_gate, t_up, t_down))


def backward_kernel(core, packed, spread_far, *refs):
    far, (d_pair, kept, sent), refs = refs[:9], refs[9:12], refs[12:]
    near, (spread, wide_rows, grad_top, sems, spread_sem) = refs[:9], refs[9:]
    normed, inv, turned, hidden_t, by_gate, by_up, t_gate, t_up, t_down = near
    first = started([(spread_far, spread)], spread_sem)
    arrived = {}
    for layer in reversed(range(normed.shape[0])):
        pairs = [(far[k].at[layer], near[k].at[layer]) for k in (3, 8, 4, 5, 2, 6, 7, 0, 1)]
        arrived[layer] = started(pairs, sems.at[layer])
    heads = packed.shape[0]
    channels = normed.shape[2]
    rows = cols = math.isqrt(normed.shape[1])
    group = packed.shape[1]
    for q in range(LANES // cols):
        piece = packed[:, :, q * cols : (q + 1) * cols].astype(WIDE)
        for h in range(heads):
            wide_rows[h * rows + q * group : h * rows + (q + 1) * group, 0:cols] = piece[h]
    waited(first)
    per_dot = LANES // heads
    for block in range(rows // per_dot):
        picked = jnp.concatenate(
            [
                wide_rows[pl.ds(block * per_dot + i, heads, stride=rows), :]
                for i in range(per_dot)
            ],
            axis=0,
        )
        top = nn(picked.T[0:cols].astype(LOW), spread[...])
        for i in range(per_dot):
            at = (block * per_dot + i) * cols
            grad_top[at : at + cols, :] = top[:, i * channels : (i + 1) * channels]
    grad = grad_top[...]
    share = 1.0 / (heads * rows)
    for layer in reversed(range(normed.shape[0])):
        low = grad.astype(LOW)
        waited(arrived[layer])
        down_sum = nn(hidden_t[layer], low)
        grad_hidden = nt(low, t_down[layer])
        grad_gate = (grad_hidden * by_gate[layer].astype(WIDE)).astype(LOW)
        grad_up = (grad_hidden * by_up[layer].astype(WIDE)).astype(LOW)
        gate_sum = nn(turned[layer], grad_gate)
        up_sum = nn(turned[layer], grad_up)
        for m, weight_sum in enumerate((gate_sum, up_sum, down_sum)):
            if weight_sum.shape[1] != LANES:
                weight_sum = jnp.concatenate(
                    [weight_sum[:, :LANES], weight_sum[:, LANES:]], axis=0
                )
            weight_sum = (weight_sum * share).astype(LOW).reshape(16, 16, LANES)

            @pl.when(core[0] == layer)
            def _(m=m, weight_sum=weight_sum):
                kept[:, m] = weight_sum

            @pl.when(core[0] != layer)
            def _(m=m, weight_sum=weight_sum):
                sent[:, m] = weight_sum

        grad_normed = nt(grad_gate, t_gate[layer]) + nt(grad_up, t_up[layer])
        unit = normed[layer]
        grad = grad + inv[layer] * (
            grad_normed
            - jnp.mean(grad_normed, axis=-1, keepdims=True)
            - unit * jnp.mean(grad_normed * unit, axis=-1, keepdims=True)
        )
    d_pair[...] = grad.astype(LOW)


def backward(core, grad_rows, spread, saved, t_gate, t_up, t_down):
    pairs, channels = saved[0].shape[1:]
    heads, rows = grad_rows.shape[0], math.isqrt(pairs)
    half = like((16, 3, 16, LANES), LOW)
    return pl.pallas_call(
        backward_kernel,
        out_shape=(like((pairs, channels), LOW), half, half),
        in_specs=[SMEM, VMEM] + [FAR] * 10,
        out_specs=[VMEM] * 3,
        scratch_shapes=[pltpu.VMEM(a.shape, a.dtype) for a in (*saved, t_gate, t_up, t_down)]
        + [
            pltpu.VMEM(spread.shape, LOW),
            pltpu.VMEM((heads * rows, LANES), WIDE),
            pltpu.VMEM((pairs, channels), WIDE),
            pltpu.SemaphoreType.DMA((t_gate.shape[0], 9)),
            pltpu.SemaphoreType.DMA((1,)),
        ],
        compiler_params=room(20),
        name="pair_backward",
    )(core, grad_rows, *far_away(spread, *saved, t_gate, t_up, t_down))


def exchange(pieces, axes):
    return lax.all_to_all(pieces, axes, 0, 0, tiled=True)


def summed(pieces):
    return jnp.sum(pieces.astype(WIDE), axis=0).astype(LOW)


def flipped(array, axis, bit):
    return lax.ppermute(array, axis, [(k, k ^ bit) for k in range(lax.axis_size(axis))])


def added(kept, received):
    return (kept.astype(WIDE) + received.astype(WIDE)).astype(LOW)


def copies(block, count):
    return jnp.broadcast_to(block, (count, *block.shape))


def finish_kernel(core, half, other, d_gate, d_up, d_down):
    def fill(layer, source):
        gate, up, down = (source[:, m].astype(WIDE).reshape(256, LANES) for m in range(3))
        d_gate[layer] = jnp.concatenate([gate[:LANES], gate[LANES:]], axis=1)
        d_up[layer] = jnp.concatenate([up[:LANES], up[LANES:]], axis=1)
        d_down[layer] = down

    for layer in range(2):

        @pl.when(core[0] == layer)
        def _(layer=layer):
            fill(layer, half)
            fill(1 - layer, other)


def finish(core, half, other):
    return pl.pallas_call(
        finish_kernel,
        out_shape=[like((2, 128, 256), WIDE), like((2, 128, 256), WIDE), like((2, 256, 128), WIDE)],
        in_specs=[SMEM] + [VMEM] * 2,
        out_specs=[VMEM] * 3,
        compiler_params=room(8),
        name="finish",
    )(core, half, other)


def sum_everywhere(core, kept, sent):
    half = added(kept, flipped(sent, "core", 1))
    block = summed(exchange(half, PLANE))
    block = summed(exchange(copies(block, 8), "z"))
    half = exchange(copies(block, 16), PLANE)
    other = flipped(half, "core", 1)
    return finish(core, half.reshape(16, 3, 16, LANES), other.reshape(16, 3, 16, LANES))


def halve_kernel(kept, received, near, away):
    half = near.shape[0]
    for k in range(2 * half):
        total = (kept[k].astype(WIDE) + received[k].astype(WIDE)).astype(LOW)
        if k < half:
            near[k] = total
        else:
            away[k - half] = total


def halve(kept, received):
    half = like((kept.shape[0] // 2, *kept.shape[1:]), LOW)
    return pl.pallas_call(
        halve_kernel,
        out_shape=(half, half),
        in_specs=[VMEM] * 2,
        out_specs=[VMEM] * 2,
        compiler_params=room(8),
        name="halve",
    )(kept, received)


def token_sum(kept, sent):
    received = flipped(sent, "yl", 1)
    for bit in (1, 2, 4):
        kept, sent = halve(kept, received)
        received = flipped(sent, "z", bit)
    return kept[0], received[0]


def per_device(
    input_tokens,
    output_cotangent,
    query_weight,
    key_weight,
    value_weight,
    output_weight,
    pair_bias,
    valid_len,
    pair_in,
    w_bias,
    t_gate,
    t_up,
    t_down,
):
    tokens = input_tokens.shape[1]
    rows, cols, channels = pair_in.shape
    heads = w_bias.shape[1]
    wq, wk, wv = query_weight.T, key_weight.T, value_weight.T
    core = lax.axis_index("core").reshape(1)
    z = lax.axis_index("z")
    place = jnp.stack([lax.axis_index("yl"), z % 2 * 4 + z // 2 % 2 * 2 + z // 4])
    part, dscores, probs, queries, keys, grads = attend(
        valid_len, input_tokens, output_cotangent, wq, wk, wv, output_weight, pair_bias[0]
    )
    received = exchange(part.reshape(16, tokens // 16, tokens), SAMP)
    kept, sent = token_pieces(place, dscores, probs, queries, keys, grads, wq, wk, wv)
    saved = forward(pair_in.reshape(rows * cols, channels), t_gate, t_up, t_down)
    per_dot = LANES // heads
    spread = jnp.einsum("ij,ch->ihjc", jnp.eye(per_dot, dtype=LOW), w_bias)
    spread = spread.reshape(LANES, per_dot * channels)
    grad_rows = exchange(bias_rows(received), HEAD)
    piece, received = token_sum(kept, sent)
    d_pair, own, other = backward(core, grad_rows, spread, saved, t_gate, t_up, t_down)
    sums = sum_everywhere(core, own.reshape(16, 48, LANES), other.reshape(16, 48, LANES))
    received, *sums = lax.optimization_barrier((received, *sums))
    d_tokens = added(piece, received).transpose(0, 2, 1)
    return (d_tokens, d_pair.reshape(rows, cols, channels), *sums)


def solution(mesh):
    torus = Mesh(mesh.devices.reshape(2, 4, 2, 2, 8), ("yh", "x", "core", "yl", "z"))
    return jax.shard_map(
        per_device,
        mesh=torus,
        in_specs=(
            P(SAMP, None, None),
            P(SAMP, None, None),
            P(None, HEAD),
            P(None, HEAD),
            P(None, HEAD),
            P(HEAD, None),
            P(HEAD, None, None),
            P(),
            P(HEAD, SAMP, None),
            P(),
            P(),
            P(),
            P(),
        ),
        out_specs=(P(SAMP, None, HEAD), P(HEAD, SAMP, None), P(), P(), P()),
        check_vma=False,
    )
```

```python
import math

import jax
import jax.numpy as jnp
from jax import lax
from jax.experimental import pallas as pl
from jax.experimental.pallas import tpu as pltpu
from jax.sharding import Mesh
from jax.sharding import PartitionSpec as P


HD = 48
SAMP = ("yh", "x", "core")
HEAD = ("yl", "z")
PLANE = ("yh", "x", "yl")
LANES = 128


EPS_NORM = 1e-05
MASKED = -1e30
LOW = jnp.bfloat16
WIDE = jnp.float32
VMEM = pl.BlockSpec(memory_space=pltpu.VMEM)
SMEM = pl.BlockSpec(memory_space=pltpu.SMEM)
FAR = pl.BlockSpec(memory_space=pltpu.HBM)


def room(mib):
    return pltpu.CompilerParams(vmem_limit_bytes=mib << 20)


def nn(a, b):
    return lax.dot_general(a, b, (((1,), (0,)), ((), ())), preferred_element_type=WIDE)


def nt(a, b):
    return lax.dot_general(a, b, (((1,), (1,)), ((), ())), preferred_element_type=WIDE)


def tn(a, b):
    return lax.dot_general(a, b, (((0,), (0,)), ((), ())), preferred_element_type=WIDE)


def like(shape, dtype):
    return jax.ShapeDtypeStruct(shape, dtype)


def far_away(*arrays):
    return [pltpu.with_memory_space_constraint(a, pltpu.HBM) for a in arrays]


def started(pairs, sems):
    moves = [pltpu.make_async_copy(a, b, sems.at[k]) for k, (a, b) in enumerate(pairs)]
    for move in moves:
        move.start()
    return moves


def waited(moves):
    for move in moves:
        move.wait()


def attend_kernel(
    valid, tokens_far, cotangent_far, wq_far, wk_far, wv_far, wo_far, bias_far,
    part_far, dscores, probs, queries_far, keys_far, grads_far,
    tokens, cotangent, wq, wk, wv, wo, bias, part, queries, keys, grads, sems, out_sems,
):
    samples, length, _ = tokens.shape
    scale = 1.0 / math.sqrt(HD)
    moves = started(
        [
            (wq_far, wq),
            (wk_far, wk),
            (wv_far, wv),
            (tokens_far.at[0], tokens.at[0]),
            (wo_far, wo),
            (cotangent_far.at[0], cotangent.at[0]),
            (tokens_far.at[1], tokens.at[1]),
            (cotangent_far.at[1], cotangent.at[1]),
            (bias_far, bias),
        ],
        sems,
    )
    rows = []
    for s in range(samples):
        waited(moves[:4] if s == 0 else moves[6:7])
        x = tokens[s]
        query, key, value = (nt(x, w[...]).astype(LOW) for w in (wq, wk, wv))
        waited(moves[4:6] if s == 0 else moves[7:8])
        grad = nt(cotangent[s], wo[...]).astype(LOW)
        queries[s], keys[s], grads[s] = query, key, grad
        rows.append((key, value))
    leaving = started(
        [(queries, queries_far), (keys, keys_far), (grads, grads_far)], out_sems.at[0]
    )
    waited(moves[8:])
    kept = lax.broadcasted_iota(jnp.int32, (length, LANES), 0) < valid[0]
    for at in range(0, length, LANES):
        block = slice(at, at + LANES)
        turned = jnp.where(kept, bias[block, :].astype(WIDE).T, MASKED)
        total = None
        for s in range(samples):
            scores = nt(rows[s][0], queries[s, block, :]) * scale + turned
            exps = jnp.exp(scores - jnp.max(scores, axis=0, keepdims=True))
            prob = exps * (1.0 / jnp.sum(exps, axis=0, keepdims=True))
            probs[s, :, block] = prob.astype(LOW)
            grad_prob = nt(rows[s][1], grads[s, block, :])
            mean = jnp.sum(prob * grad_prob, axis=0, keepdims=True)
            dscore = prob * (grad_prob - mean)
            dscores[s, :, block] = dscore.astype(LOW)
            total = dscore if total is None else total + dscore
        part[:, block] = total.astype(LOW)
        leaving += started([(part.at[:, block], part_far.at[:, block])], out_sems.at[1, at // LANES :])
    waited(leaving)


def attend(valid, tokens, cotangent, wq, wk, wv, wo, bias):
    samples, length, _ = tokens.shape
    square = like((samples, length, length), LOW)
    heads = pltpu.HBM((samples, length, HD), LOW)
    return pl.pallas_call(
        attend_kernel,
        out_shape=(pltpu.HBM((length, length), LOW), square, square, heads, heads, heads),
        in_specs=[SMEM] + [FAR] * 7,
        out_specs=[FAR] + [VMEM] * 2 + [FAR] * 3,
        scratch_shapes=[
            pltpu.VMEM(a.shape, LOW) for a in (tokens, cotangent, wq, wk, wv, wo, bias)
        ]
        + [pltpu.VMEM((length, length), LOW)]
        + [pltpu.VMEM((samples, length, HD), LOW)] * 3
        + [pltpu.SemaphoreType.DMA((9,)), pltpu.SemaphoreType.DMA((2, 4))],
        compiler_params=room(16),
        name="attend",
    )(valid, *far_away(tokens, cotangent, wq, wk, wv, wo, bias))


def token_kernel(place, dscores, probs, *refs):
    far, (kept, sent), near, sems = refs[:6], refs[6:8], refs[8:14], refs[14]
    queries, keys, grads, wq, wk, wv = near
    waited(started(list(zip(far, near)), sems))
    scale = 1.0 / math.sqrt(HD)
    weight = jnp.concatenate([wq[...], wk[...], wv[...]], axis=0)
    for s in range(dscores.shape[0]):
        d = dscores[s]
        joined = jnp.concatenate(
            [
                (nn(keys[s].T, d) * scale).astype(LOW),
                (nt(queries[s].T, d) * scale).astype(LOW),
                nt(grads[s].T, probs[s]).astype(LOW),
            ],
            axis=0,
        )
        terms = tn(weight, joined).astype(LOW)
        for r in range(16):
            z = r % 8
            slot = (z % 2 * 4 + z // 2 % 2 * 2 + z // 4) ^ place[1]
            piece = terms[r * HD : (r + 1) * HD]

            @pl.when(place[0] == r // 8)
            def _(slot=slot, piece=piece):
                kept[slot, s] = piece

            @pl.when(place[0] != r // 8)
            def _(slot=slot, piece=piece):
                sent[slot, s] = piece


def token_pieces(place, dscores, probs, queries, keys, grads, wq, wk, wv):
    samples, length, _ = dscores.shape
    half = pltpu.HBM((8, samples, HD, length), LOW)
    return pl.pallas_call(
        token_kernel,
        out_shape=(half, half),
        in_specs=[SMEM] + [VMEM] * 2 + [FAR] * 6,
        out_specs=[VMEM] * 2,
        scratch_shapes=[pltpu.VMEM(a.shape, LOW) for a in (queries, keys, grads, wq, wk, wv)]
        + [pltpu.SemaphoreType.DMA((6,))],
        compiler_params=room(16),
        name="token_pieces",
    )(place, dscores, probs, *far_away(queries, keys, grads, wq, wk, wv))


def rows_kernel(pieces, out):
    total = pieces[0].astype(WIDE)
    for k in range(1, pieces.shape[0]):
        total = total + pieces[k].astype(WIDE)
    turned = total.T.reshape(out.shape[0], LANES // total.shape[0], -1, total.shape[0])
    packed = jnp.concatenate([turned[:, q] for q in range(turned.shape[1])], axis=-1)
    out[...] = packed.astype(LOW)


def bias_rows(pieces):
    count, cols, length = pieces.shape
    return pl.pallas_call(
        rows_kernel,
        out_shape=like((count, length // count * cols // LANES, LANES), LOW),
        in_specs=[VMEM],
        out_specs=VMEM,
        compiler_params=room(4),
        name="bias_rows_sum",
    )(pieces)


def forward_step(field, gate_weight, up_weight):
    centred = field - jnp.mean(field, axis=-1, keepdims=True)
    variance = jnp.mean(centred * centred, axis=-1, keepdims=True)
    inv_std = lax.rsqrt(variance + EPS_NORM)
    unit = centred * inv_std
    low = unit.astype(LOW)
    gate = nn(low, gate_weight)
    up = nn(low, up_weight)
    sig = jax.nn.sigmoid(gate)
    act = gate * sig
    hidden = (act * up).astype(LOW)
    saved = (
        unit,
        jnp.broadcast_to(inv_std, unit.shape),
        low.T,
        hidden.T,
        (up * (sig * (1.0 + gate * (1.0 - sig)))).astype(LOW),
        act.astype(LOW),
    )
    return saved, hidden


def first_kernel(pair_far, t_gate_far, t_up_far, t_down_far, *refs):
    far, (pair, t_gate, t_up, t_down, *near, in_sems, out_sems) = refs[:7], refs[7:]
    waited(
        started(
            [
                (pair_far, pair),
                (t_gate_far.at[0], t_gate),
                (t_up_far.at[0], t_up),
                (t_down_far.at[0], t_down),
            ],
            in_sems,
        )
    )
    field = pair[...].astype(WIDE)
    saved, hidden = forward_step(field, t_gate[...], t_up[...])
    for ref, value in zip(near, saved):
        ref[...] = value
    moves = started(list(zip(near[:6], far[:6])), out_sems)
    near[6][...] = field + nn(hidden, t_down[...])
    waited(moves + started([(near[6], far[6])], out_sems.at[6:]))


def second_kernel(field_far, t_gate_far, t_up_far, *refs):
    far, out, (field, t_gate, t_up, *near, in_sems, out_sems) = refs[:2], refs[2:6], refs[6:]
    waited(
        started(
            [(field_far, field), (t_gate_far.at[1], t_gate), (t_up_far.at[1], t_up)], in_sems
        )
    )
    saved, _ = forward_step(field[...], t_gate[...], t_up[...])
    for ref, value in zip((*near, *out), saved):
        ref[...] = value
        if ref is near[1]:
            moves = started(list(zip(near, far)), out_sems)
    waited(moves)


def saved_shapes(pairs, channels, width):
    return (
        ((pairs, channels), WIDE),
        ((pairs, channels), WIDE),
        ((channels, pairs), LOW),
        ((width, pairs), LOW),
        ((pairs, width), LOW),
        ((pairs, width), LOW),
    )


def forward_first(pair, t_gate, t_up, t_down):
    shapes = (*saved_shapes(*pair.shape, t_gate.shape[2]), (pair.shape, WIDE))
    *saved, field = pl.pallas_call(
        first_kernel,
        out_shape=[pltpu.HBM(*a) for a in shapes],
        in_specs=[FAR] * 4,
        out_specs=[FAR] * 7,
        scratch_shapes=[
            pltpu.VMEM(a, LOW)
            for a in (pair.shape, t_gate.shape[1:], t_up.shape[1:], t_down.shape[1:])
        ]
        + [pltpu.VMEM(*a) for a in shapes]
        + [pltpu.SemaphoreType.DMA((4,)), pltpu.SemaphoreType.DMA((7,))],
        compiler_params=room(24),
        name="pair_forward_0",
    )(*far_away(pair, t_gate, t_up, t_down))
    return saved, field


def forward_second(field, t_gate, t_up):
    shapes = saved_shapes(*field.shape, t_gate.shape[2])
    return pl.pallas_call(
        second_kernel,
        out_shape=[pltpu.HBM(*a) for a in shapes[:2]] + [like(*a) for a in shapes[2:]],
        in_specs=[FAR] * 3,
        out_specs=[FAR] * 2 + [VMEM] * 4,
        scratch_shapes=[
            pltpu.VMEM(field.shape, WIDE),
            pltpu.VMEM(t_gate.shape[1:], LOW),
            pltpu.VMEM(t_up.shape[1:], LOW),
            pltpu.VMEM(*shapes[0]),
            pltpu.VMEM(*shapes[1]),
            pltpu.SemaphoreType.DMA((3,)),
            pltpu.SemaphoreType.DMA((2,)),
        ],
        compiler_params=room(16),
        name="pair_forward_1",
    )(*far_away(field, t_gate, t_up))


def backward_kernel(core, packed, *refs):
    last, far, (d_pair, kept, sent), refs = refs[:4], refs[4:16], refs[16:19], refs[19:]
    near, (wide_rows, grad_top, spread, sems) = refs[:12], refs[12:]
    w_bias, t_down, t_gate, t_up = near[:4]
    moves = started(list(zip(far, near)), sems)
    heads = packed.shape[0]
    pairs, channels = grad_top.shape
    rows = cols = math.isqrt(pairs)
    group = packed.shape[1]
    for q in range(LANES // cols):
        piece = packed[:, :, q * cols : (q + 1) * cols].astype(WIDE)
        for h in range(heads):
            wide_rows[h * rows + q * group : h * rows + (q + 1) * group, 0:cols] = piece[h]
    per_dot = LANES // heads
    spread[...] = jnp.zeros(spread.shape, LOW)
    waited(moves[:1])
    for i in range(per_dot):
        spread[i * heads : (i + 1) * heads, i * channels : (i + 1) * channels] = w_bias[...]
    for block in range(rows // per_dot):
        picked = jnp.concatenate(
            [
                wide_rows[pl.ds(block * per_dot + i, heads, stride=rows), :]
                for i in range(per_dot)
            ],
            axis=0,
        )
        top = nn(picked.T[0:cols].astype(LOW), spread[...])
        for i in range(per_dot):
            at = (block * per_dot + i) * cols
            grad_top[at : at + cols, :] = top[:, i * channels : (i + 1) * channels]
    grad = grad_top[...]
    share = 1.0 / (heads * rows)
    for layer in (1, 0):
        normed, inv, turned, hidden_t, by_gate, by_up = (*near[4:6], *last) if layer else near[6:]
        low = grad.astype(LOW)
        waited(moves[1:2] if layer else moves[6:])
        down_sum = nn(hidden_t[...], low)
        grad_hidden = nt(low, t_down[layer])
        grad_gate = (grad_hidden * by_gate[...].astype(WIDE)).astype(LOW)
        grad_up = (grad_hidden * by_up[...].astype(WIDE)).astype(LOW)
        waited(moves[2:4] if layer else [])
        gate_sum = nn(turned[...], grad_gate)
        up_sum = nn(turned[...], grad_up)
        for m, weight_sum in enumerate((gate_sum, up_sum, down_sum)):
            if weight_sum.shape[1] != LANES:
                weight_sum = jnp.concatenate(
                    [weight_sum[:, :LANES], weight_sum[:, LANES:]], axis=0
                )
            weight_sum = (weight_sum * share).astype(LOW).reshape(16, 16, LANES)

            @pl.when(core[0] == layer)
            def _(m=m, weight_sum=weight_sum):
                kept[:, m] = weight_sum

            @pl.when(core[0] != layer)
            def _(m=m, weight_sum=weight_sum):
                sent[:, m] = weight_sum

        grad_normed = nt(grad_gate, t_gate[layer]) + nt(grad_up, t_up[layer])
        waited(moves[4:6] if layer else [])
        unit = normed[...]
        grad = grad + inv[...] * (
            grad_normed
            - jnp.mean(grad_normed, axis=-1, keepdims=True)
            - unit * jnp.mean(grad_normed * unit, axis=-1, keepdims=True)
        )
    d_pair[...] = grad.astype(LOW)


def backward(core, grad_rows, w_bias, first, last, t_gate, t_up, t_down):
    pairs, channels = last[0].shape
    heads, rows = grad_rows.shape[0], math.isqrt(pairs)
    half = like((16, 3, 16, LANES), LOW)
    far = (w_bias, t_down, t_gate, t_up, *last[:2], *first)
    return pl.pallas_call(
        backward_kernel,
        out_shape=(like((pairs, channels), LOW), half, half),
        in_specs=[SMEM] + [VMEM] * 5 + [FAR] * 12,
        out_specs=[VMEM] * 3,
        scratch_shapes=[pltpu.VMEM(a.shape, a.dtype) for a in far]
        + [
            pltpu.VMEM((heads * rows, LANES), WIDE),
            pltpu.VMEM((pairs, channels), WIDE),
            pltpu.VMEM((LANES, LANES // heads * channels), LOW),
            pltpu.SemaphoreType.DMA((12,)),
        ],
        compiler_params=room(20),
        name="pair_backward",
    )(core, grad_rows, *last[2:], *far_away(*far))


def exchange(pieces, axes):
    return lax.all_to_all(pieces, axes, 0, 0, tiled=True)


def summed(pieces):
    return jnp.sum(pieces.astype(WIDE), axis=0).astype(LOW)


def flipped(array, axis, bit):
    return lax.ppermute(array, axis, [(k, k ^ bit) for k in range(lax.axis_size(axis))])


def added(kept, received):
    return (kept.astype(WIDE) + received.astype(WIDE)).astype(LOW)


def copies(block, count):
    return jnp.broadcast_to(block, (count, *block.shape))


def finish_kernel(core, half, other, piece, received, d_gate, d_up, d_down, d_tokens):
    def fill(layer, source):
        gate, up, down = (source[:, m].astype(WIDE).reshape(256, LANES) for m in range(3))
        d_gate[layer] = jnp.concatenate([gate[:LANES], gate[LANES:]], axis=1)
        d_up[layer] = jnp.concatenate([up[:LANES], up[LANES:]], axis=1)
        d_down[layer] = down

    for layer in range(2):

        @pl.when(core[0] == layer)
        def _(layer=layer):
            fill(layer, half)
            fill(1 - layer, other)

    d_tokens[...] = (piece[...].astype(WIDE) + received[...].astype(WIDE)).astype(LOW)


def finish(core, half, other, piece, received):
    return pl.pallas_call(
        finish_kernel,
        out_shape=[
            like((2, 128, 256), WIDE),
            like((2, 128, 256), WIDE),
            like((2, 256, 128), WIDE),
            like(piece.shape, LOW),
        ],
        in_specs=[SMEM] + [VMEM] * 4,
        out_specs=[VMEM] * 4,
        compiler_params=room(8),
        name="finish",
    )(core, half, other, piece, received)


def sum_everywhere(kept, sent):
    half = added(kept, flipped(sent, "core", 1))
    block = summed(exchange(half, PLANE))
    block = summed(exchange(copies(block, 8), "z"))
    half = exchange(copies(block, 16), PLANE)
    other = flipped(half, "core", 1)
    return half.reshape(16, 3, 16, LANES), other.reshape(16, 3, 16, LANES)


def halve_kernel(kept, received, near, away):
    half = near.shape[0]
    for k in range(2 * half):
        total = (kept[k].astype(WIDE) + received[k].astype(WIDE)).astype(LOW)
        if k < half:
            near[k] = total
        else:
            away[k - half] = total


def halve(kept, received):
    half = like((kept.shape[0] // 2, *kept.shape[1:]), LOW)
    return pl.pallas_call(
        halve_kernel,
        out_shape=(half, half),
        in_specs=[VMEM] * 2,
        out_specs=[VMEM] * 2,
        compiler_params=room(8),
        name="halve",
    )(kept, received)


def token_sum(kept, sent):
    received = flipped(sent, "yl", 1)
    for bit in (1, 2, 4):
        kept, sent = halve(kept, received)
        received = flipped(sent, "z", bit)
    return kept[0], received[0]


def per_device(
    input_tokens,
    output_cotangent,
    query_weight,
    key_weight,
    value_weight,
    output_weight,
    pair_bias,
    valid_len,
    pair_in,
    w_bias,
    t_gate,
    t_up,
    t_down,
):
    tokens = input_tokens.shape[1]
    rows, cols, channels = pair_in.shape
    wq, wk, wv = query_weight.T, key_weight.T, value_weight.T
    core = lax.axis_index("core").reshape(1)
    z = lax.axis_index("z")
    place = jnp.stack([lax.axis_index("yl"), z % 2 * 4 + z // 2 % 2 * 2 + z // 4])
    part, dscores, probs, queries, keys, grads = attend(
        valid_len, input_tokens, output_cotangent, wq, wk, wv, output_weight, pair_bias[0]
    )
    received = exchange(part.reshape(16, tokens // 16, tokens), SAMP)
    kept, sent = token_pieces(place, dscores, probs, queries, keys, grads, wq, wk, wv)
    first, field = forward_first(pair_in.reshape(rows * cols, channels), t_gate, t_up, t_down)
    last = forward_second(field, t_gate, t_up)
    grad_rows = exchange(bias_rows(received), HEAD)
    piece, received = token_sum(kept, sent)
    d_pair, own, other = backward(core, grad_rows, w_bias.T, first, last, t_gate, t_up, t_down)
    half, other = sum_everywhere(own.reshape(16, 48, LANES), other.reshape(16, 48, LANES))
    *sums, d_tokens = finish(core, half, other, piece, received)
    return (d_tokens.transpose(0, 2, 1), d_pair.reshape(rows, cols, channels), *sums)


def solution(mesh):
    torus = Mesh(mesh.devices.reshape(2, 4, 2, 2, 8), ("yh", "x", "core", "yl", "z"))
    return jax.shard_map(
        per_device,
        mesh=torus,
        in_specs=(
            P(SAMP, None, None),
            P(SAMP, None, None),
            P(None, HEAD),
            P(None, HEAD),
            P(None, HEAD),
            P(HEAD, None),
            P(HEAD, None, None),
            P(),
            P(HEAD, SAMP, None),
            P(),
            P(),
            P(),
            P(),
        ),
        out_specs=(P(SAMP, None, HEAD), P(HEAD, SAMP, None), P(), P(), P()),
        check_vma=False,
    )
```
